32 devices in a mesh: blk: 8 (over z, y), aux: 4 (over x, core).
Axes of the slice: x: 2, y: 2, z: 4, core: 2. Of those that a mesh axis runs over, the one named last changes fastest.
Arguments:
- adjoint: bfloat16 [1024, 1024], P(('blk', 'aux')), may hold values from -0.1875 to 0.1875
- three_centre: bfloat16 [128, 32, 32, 1024], P(('blk', 'aux')), may hold values from -1 to 1
- occ_density: bfloat16 [64, 1024], P('blk'), may hold values from -1 to 1
- vir_density: bfloat16 [64, 1024], P('blk'), may hold values from -1 to 1
- block_sizes: int32 [64], P('blk'), may hold values from 16 to 32
- tile_rows: int32 [128], P(('blk', 'aux')), may hold values from 0 to 7
- col_owner: int32 [128, 1], P(('blk', 'aux')), may hold values from 0 to 7; in each aligned block of 16 rows (0 to 15, 16 to 31, ...) at most 4 rows name the same one
- col_block: int32 [128], P(('blk', 'aux')), may hold values from 0 to 7
Outputs:
- occ_grad: float32 [64, 1024], P(('blk', 'aux'))
- vir_grad: float32 [64, 1024], P(('blk', 'aux'))
The draws below stay inside these ranges and needn't reach their ends.
Inputs may be any that keep to these rules, and one draw needn't show every extreme that they name: `col_owner`: among the 16 tiles of one blk index (aligned blocks of 16 tiles), at most 4 name the same owner, and some blk index reaches 4.
All inputs are finite; a program needn't handle non-finite values.
Results may differ from the reference program's by a relative error of at most 0.0041.
Values may be sent and summed in bfloat16 or wider, within the bound.
A program may use at most 128 MiB of HBM per device.

```python
import math
import jax
import jax.numpy as jnp
import numpy as np
from jax import lax

BS = 32
NAUX = 1024
BLK_DEV = 8
TILE_DEV = 4
TILES_ROW = 16
CAP = 4
NB = 64
NTILE = 128
N_BLK = 8


def plant(values, stream_key, smallest, top_value):
    longest = values.shape.index(max(values.shape))
    spots = []
    for shift in (0, 1):
        where = [jax.random.randint(jax.random.fold_in(stream_key, axis), (), 0, length) for axis, length in enumerate(values.shape)]
        where[longest] = (where[longest] + shift) % values.shape[longest]
        spots.append(tuple(where))
    return values.at[spots[0]].set(smallest).at[spots[1]].set(top_value)


def block_scale(key, dims, shards, low, high):
    def one(axis_at, parts):
        heights = jax.random.uniform(jax.random.fold_in(jax.random.fold_in(key, 6), axis_at), (parts,), jnp.float32, low / len(shards), high / len(shards))
        return jnp.repeat(jnp.exp(heights), dims[axis_at] // parts).reshape((-1,) + (1,) * (len(dims) - axis_at - 1))

    level = one(*shards[0])
    for cut in shards[1:]:
        level = level * one(*cut)
    return level


def assign_block(rng, own, number, rows, amount, top, most, slope):
    order = jax.random.permutation(rng, amount)
    packed, ordinary = portions_of(amount, rows * top, most, slope, True), portions_of(amount, rows * top, most, slope, False)
    places = jnp.arange(amount)

    def named(tallies, rotation):
        used = int((tallies > 0).sum())
        fixed = max(1, used // 4)
        shifted = fixed + (places - fixed + rotation * (used - fixed)) % max(1, amount - fixed)
        return jnp.zeros((amount,), jnp.int32).at[order[jnp.where(places < fixed, places, shifted)]].set(jnp.asarray(tallies, jnp.int32))

    tallies = jnp.where(number % 4 == 0, named(packed, number // 4), named(ordinary, number - number // 4 - 1))
    mixed = jax.random.permutation(jax.random.fold_in(own, 3), amount)
    source_of, taker = mixed[0:amount // 2 * 2:2], mixed[1:amount // 2 * 2:2]
    slack = jnp.minimum(tallies[source_of] - 1, most - tallies[taker]) // 2
    slack = jnp.where((source_of == order[0]) | (taker == order[0]) | (tallies[taker] == 0), 0, jnp.maximum(slack, 0))
    shifted = jax.random.randint(jax.random.fold_in(own, 4), (amount // 2,), 0, 1 << 20) % (slack + 1)
    tallies = tallies.at[source_of].add(-shifted).at[taker].add(shifted)
    items = jnp.searchsorted(jnp.cumsum(tallies), jnp.arange(rows * top), side="right").astype(jnp.int32)
    listing = items.reshape(top, rows).T
    listing = listing[jax.random.permutation(jax.random.fold_in(own, 1), rows)]
    rotation = jax.random.randint(jax.random.fold_in(own, 2), (rows, 1), 0, top)
    return jnp.take_along_axis(listing, (jnp.arange(top)[None, :] + rotation) % top, axis=1)


def portions_of(count, total, limit, slope, full):
    portions = [(1 << 20) // math.isqrt(rank ** slope) + 1 for rank in range(1, count + 1)]
    largest = limit if full else min(limit, max(-(-total // count), total * portions[0] // sum(portions)))
    least = 1 if total - largest >= count - 1 else 0
    counts, spare = [largest] + [least] * (count - 1), total - largest - least * (count - 1)
    while spare > 0:
        movable = [i for i in range(1, count) if counts[i] < largest] or [i for i in range(1, count) if counts[i] < limit]
        pool, budget = sum([portions[i] for i in movable]), spare
        for i in movable:
            extra = min(limit - counts[i], max(1, budget * portions[i] // pool), spare)
            counts[i] = counts[i] + extra
            spare = spare - extra
    return np.array(counts)


def bell_draw(stream_key, dims, width, bound, split=(), held_as=jnp.bfloat16):
    level = block_scale(stream_key, dims, split, -0.22, 0.18) if split else 1.0
    entries = jax.random.normal(stream_key, dims, jnp.float32) * width * level
    return jnp.minimum(jnp.maximum(entries, -bound), bound).astype(held_as)


def setup_inputs(seed: int = 0) -> dict:
    key_of = jax.random.split(jax.random.key(seed), 9)
    adjoint = bell_draw(key_of[0], (NAUX, NAUX), NAUX ** -0.5, 0.1875, ((0, 32),))
    three_centre = bell_draw(key_of[1], (NTILE, BS, BS, NAUX), BS ** -0.5, 1.0, ((0, 32),))
    occ_density = bell_draw(key_of[2], (NB, BS * BS), BS ** -0.5, 1.0, ((0, 8),))
    vir_density = bell_draw(key_of[3], (NB, BS * BS), BS ** -0.5, 1.0, ((0, 8),))
    block_sizes = plant(jax.random.randint(key_of[4], (NB,), BS // 2, BS + 1), jax.random.fold_in(key_of[4], 1), BS // 2, BS).astype(jnp.int32)
    tile_rows = plant(jax.random.randint(key_of[5], (NTILE,), 0, BLK_DEV), jax.random.fold_in(key_of[5], 1), 0, BLK_DEV - 1).astype(jnp.int32)
    col_owner_keys = jax.random.split(jax.random.fold_in(key_of[6], 1), NTILE // TILES_ROW)
    col_owner_turns = jax.random.permutation(jax.random.fold_in(key_of[6], 3), NTILE // TILES_ROW)
    col_owner = jax.vmap(lambda own, number: assign_block(jax.random.fold_in(key_of[6], 2), own, number, TILES_ROW, N_BLK, 1, CAP, 2))(col_owner_keys, col_owner_turns).reshape((NTILE, 1))
    col_block = plant(jax.random.randint(key_of[7], (NTILE,), 0, BLK_DEV), jax.random.fold_in(key_of[7], 1), 0, BLK_DEV - 1).astype(jnp.int32)
    return dict(adjoint=adjoint, three_centre=three_centre, occ_density=occ_density, vir_density=vir_density, block_sizes=block_sizes, tile_rows=tile_rows, col_owner=col_owner, col_block=col_block)


def reference(adjoint, three_centre, occ_density, vir_density, block_sizes, tile_rows, col_owner, col_block):
    func_index = jnp.arange(BS, dtype=jnp.int32)
    live_funcs = (func_index[None, :] < block_sizes[:, None]).astype(jnp.float32)
    live_pairs = (live_funcs[:, :, None] * live_funcs[:, None, :]).reshape(NB, BS * BS)
    occ_masked = (occ_density.astype(jnp.float32) * live_pairs).astype(jnp.bfloat16)
    vir_masked = (vir_density.astype(jnp.float32) * live_pairs).astype(jnp.bfloat16)
    tile_ids = jnp.arange(NTILE, dtype=jnp.int32)
    row_ids = ((tile_ids // TILES_ROW) * BLK_DEV + tile_rows).astype(jnp.int32)
    col_ids = (col_owner[:, 0] * BLK_DEV + col_block).astype(jnp.int32)
    adjoint_t = adjoint.T

    def one_group(totals, group_id):
        occ_acc, vir_acc = totals
        first = (group_id * TILE_DEV).astype(jnp.int32)
        tile_group = lax.dynamic_slice_in_dim(three_centre, first, TILE_DEV, 0)
        group_rows = lax.dynamic_slice_in_dim(row_ids, first, TILE_DEV, 0)
        group_cols = lax.dynamic_slice_in_dim(col_ids, first, TILE_DEV, 0)
        tile_flat = tile_group.reshape(TILE_DEV * BS * BS, NAUX)
        contracted = jnp.dot(tile_flat, adjoint_t, preferred_element_type=jnp.float32).astype(jnp.bfloat16)
        contracted = contracted.reshape(TILE_DEV, BS, BS, NAUX).astype(jnp.float32)
        vir_tile_d = vir_masked[group_cols].reshape(TILE_DEV, BS, BS).astype(jnp.float32)
        occ_tile_d = occ_masked[group_rows].reshape(TILE_DEV, BS, BS).astype(jnp.float32)
        tiles_f = tile_group.astype(jnp.float32)
        weighted = jnp.einsum('tjk,tijq->tikq', vir_tile_d, contracted).astype(jnp.bfloat16).astype(jnp.float32)
        occ_tile = jnp.einsum('tikq,tlkq->til', weighted, tiles_f)
        rotated = jnp.einsum('tij,tjkq->tikq', occ_tile_d, tiles_f).astype(jnp.bfloat16).astype(jnp.float32)
        vir_tile = jnp.einsum('tijq,tikq->tjk', contracted, rotated)
        occ_acc = occ_acc.at[group_rows].add(occ_tile.reshape(TILE_DEV, BS * BS))
        vir_acc = vir_acc.at[group_cols].add(vir_tile.reshape(TILE_DEV, BS * BS))
        return (occ_acc, vir_acc), None

    zeros = jnp.zeros((NB, BS * BS), jnp.float32)
    (occ_acc, vir_acc), _ = lax.scan(one_group, (zeros, zeros), jnp.arange(NTILE // TILE_DEV, dtype=jnp.int32))
    norm_factor = NAUX ** -0.5
    return occ_acc * live_pairs * norm_factor, vir_acc * live_pairs * norm_factor
```

```python
import functools

import jax
import jax.numpy as jnp
from jax import lax
from jax.experimental import pallas as pl
from jax.experimental.pallas import tpu as pltpu
from jax.sharding import PartitionSpec as P

BS = 32
CHUNK = 256
MESH = pl.DeviceIdType.MESH
F32 = jnp.float32
BF16 = jnp.bfloat16


def iota(shape, dim):
    return lax.broadcasted_iota(jnp.int32, shape, dim)


def gather_kernel(depth, pay_ref, out_ref, send_sem, recv_sem, own_sem):
    b = lax.axis_index("blk")
    a = lax.axis_index("aux")
    z, y, x, c = b // 2, b % 2, a // 2, a % 2
    up, down, over_x, over_y, mate = range(5)
    place = {
        up: (b + 2, a),
        down: (b - 2, a),
        over_x: (b, (1 - x) * 2 + c),
        over_y: (z * 2 + 1 - y, a),
        mate: (b, x * 2 + 1 - c),
    }
    has_up, has_down = z < depth - 1, z > 0

    def ident(xx, yy, zz, cc):
        return ((zz * 2 + yy) * 2 + xx) * 2 + cc

    me = ident(x, y, z, c)
    barrier = pltpu.get_barrier_semaphore()
    for way in (over_x, over_y, mate):
        pl.semaphore_signal(barrier, inc=1, device_id=place[way], device_id_type=MESH)

    @pl.when(has_up)
    def _():
        pl.semaphore_signal(barrier, inc=1, device_id=place[up], device_id_type=MESH)

    @pl.when(has_down)
    def _():
        pl.semaphore_signal(barrier, inc=1, device_id=place[down], device_id_type=MESH)

    own = pltpu.make_async_copy(pay_ref, out_ref.at[me], own_sem)
    own.start()
    pl.semaphore_wait(barrier, 3 + has_up.astype(jnp.int32) + has_down.astype(jnp.int32))

    def copy(way, block, src=None):
        return pltpu.make_async_remote_copy(
            src_ref=out_ref.at[block] if src is None else src,
            dst_ref=out_ref.at[block],
            send_sem=send_sem.at[way, block],
            recv_sem=recv_sem.at[block],
            device_id=place[way],
            device_id_type=MESH,
        )

    def send(way, block, src=None, when=None):
        if when is None:
            copy(way, block, src).start()
        else:

            @pl.when(when)
            def _():
                copy(way, block, src).start()

    def arrive(block):
        copy(mate, block).wait_recv()

    send(up, me, pay_ref, has_up)
    send(down, me, pay_ref, has_down)
    send(over_x, me, pay_ref)
    send(over_y, me, pay_ref)
    send(mate, me, pay_ref)

    def column(zz, from_up):
        block = ident(x, y, zz, c)
        arrive(block)
        if from_up:
            send(down, block, when=has_down)
        else:
            send(up, block, when=has_up)
        send(over_x, block)
        send(over_y, block)
        send(mate, block)

    def sides(zz):
        block = ident(1 - x, y, zz, c)
        arrive(block)
        send(over_y, block, when=zz % 2 == 0)
        send(mate, block)
        block = ident(x, 1 - y, zz, c)
        arrive(block)
        send(over_x, block, when=zz % 2 == 1)
        send(mate, block)

    def corner(zz):
        block = ident(1 - x, 1 - y, zz, c)
        arrive(block)
        send(mate, block)

    def planes(dist, work):
        if dist == 0:
            work(z, None)
        elif 0 < dist < depth:

            @pl.when(z + dist < depth)
            def _():
                work(z + dist, True)

            @pl.when(z - dist >= 0)
            def _():
                work(z - dist, False)

    for step in range(1, depth + 2):
        planes(step, column)
        planes(step - 1, lambda zz, _: sides(zz))
        if step >= 2:
            planes(step - 2, lambda zz, _: corner(zz))

    own.wait()
    for zz in range(depth):
        for xx in (x, 1 - x):
            for yy in (y, 1 - y):
                arrive(ident(xx, yy, zz, 1 - c))
    for zz in range(depth):
        block = ident(x, y, zz, c)
        for way in (over_x, over_y, mate):
            copy(way, block).wait_send()

        @pl.when((zz <= z) & has_up)
        def _():
            copy(up, ident(x, y, zz, c)).wait_send()

        @pl.when((zz >= z) & has_down)
        def _():
            copy(down, ident(x, y, zz, c)).wait_send()

        block = ident(1 - x, y, zz, c)
        copy(mate, block).wait_send()
        if zz % 2 == 0:
            copy(over_y, block).wait_send()
        block = ident(x, 1 - y, zz, c)
        copy(mate, block).wait_send()
        if zz % 2 == 1:
            copy(over_x, block).wait_send()
        copy(mate, ident(1 - x, 1 - y, zz, c)).wait_send()


def gather(payload, n_blk, n_aux):
    n_dev = n_blk * n_aux
    if n_aux != 4 or n_blk % 2:
        return lax.all_gather(payload, ("blk", "aux"), axis=0)
    return pl.pallas_call(
        functools.partial(gather_kernel, n_blk // 2),
        out_shape=jax.ShapeDtypeStruct((n_dev,) + payload.shape, payload.dtype),
        in_specs=[pl.BlockSpec(memory_space=pltpu.VMEM)],
        out_specs=pl.BlockSpec(memory_space=pltpu.VMEM),
        scratch_shapes=[
            pltpu.SemaphoreType.DMA((5, n_dev)),
            pltpu.SemaphoreType.DMA((n_dev,)),
            pltpu.SemaphoreType.DMA,
        ],
        compiler_params=pltpu.CompilerParams(collective_id=0, has_side_effects=True),
        name="gather",
    )(payload)


def tile_kernel(
    n_aux, own, sizes, rows, owners, blocks, occ_ref, vir_ref, adj_ref, t_ref, occ_out, vir_out, vir_acc
):
    t = pl.program_id(0)
    pairs = BS * BS
    naux = adj_ref.shape[0]

    @pl.when(t == 0)
    def _():
        occ_out[...] = jnp.zeros_like(occ_out)
        vir_acc[...] = jnp.zeros_like(vir_acc)

    row, owner, block = rows[t], owners[t], blocks[t]
    size = sizes[row]
    lane = iota((1, pairs), 1)
    inside = (lane // BS < size) & (lane % BS < size)
    occ_all = occ_ref[...].astype(F32)
    occ_row = jnp.sum(jnp.where(iota(occ_all.shape, 0) == row, occ_all, 0.0), axis=0, keepdims=True)
    occ_row = jnp.where(inside, occ_row, 0.0)
    home = owner * n_aux + block // own
    vir_all = vir_ref[home].astype(F32)
    vir_row = jnp.sum(jnp.where(iota(vir_all.shape, 0) == block % own, vir_all, 0.0), axis=0, keepdims=True)
    diag = iota((BS, pairs), 1) // BS == iota((BS, pairs), 0)
    fold_minor = (iota((pairs, 128), 0) % BS == iota((pairs, 128), 1) % BS).astype(BF16)
    fold_major = (iota((pairs, 128), 0) // BS == iota((pairs, 128), 1) % BS).astype(BF16)
    spread = (iota((128, pairs), 0) == iota((128, pairs), 1) // BS).astype(BF16)
    repeat = pairs // 128

    def square(flat):
        return jnp.dot(jnp.where(diag, flat, 0.0).astype(BF16), fold_minor, preferred_element_type=F32)

    occ_rep = jnp.dot(square(occ_row).astype(BF16), spread, preferred_element_type=F32)
    vir_rep = jnp.concatenate([square(vir_row)] * repeat, axis=1)

    nt = (((1,), (1,)), ((), ()))
    acc = jnp.zeros((BS, pairs), F32)
    lines = []
    for first in range(0, pairs, CHUNK):
        part = lax.dot_general(t_ref[0, first : first + CHUNK, :], adj_ref[...], nt, preferred_element_type=F32)
        gram = lax.dot_general(part.astype(BF16), t_ref[0], nt, preferred_element_type=F32)
        for at in range(CHUNK // BS):
            i = first // BS + at
            block_i = gram[at * BS : (at + 1) * BS, :]
            acc = acc + block_i * occ_rep[i : i + 1, :]
            lines.append(jnp.sum(block_i * vir_rep, axis=0, keepdims=True))
    zmat = jnp.concatenate(lines, axis=0)

    def flatten(mat, fold):
        high = mat.astype(BF16)
        low = (mat - high.astype(F32)).astype(BF16)
        both = jnp.dot(high, fold, preferred_element_type=F32) + jnp.dot(low, fold, preferred_element_type=F32)
        wide = jnp.concatenate([both] * repeat, axis=1)
        return jnp.sum(jnp.where(diag, wide, 0.0), axis=0, keepdims=True)

    occ_flat = flatten(zmat, fold_major)
    vir_flat = flatten(acc, fold_minor)
    slot = iota((own, pairs), 0)
    occ_out[row // own] = occ_out[row // own] + jnp.where(slot == row % own, occ_flat, 0.0)
    vir_acc[home] = vir_acc[home] + jnp.where(slot == block % own, vir_flat, 0.0)

    @pl.when(t == pl.num_programs(0) - 1)
    def _():
        vir_out[...] = vir_acc[...].astype(vir_out.dtype)


def tiles(sizes, rows, owners, blocks, occ, vir, adj, three, n_dev, n_aux):
    count, pairs, naux = three.shape
    own = occ.shape[0] // n_aux
    smem = pl.BlockSpec(memory_space=pltpu.SMEM)
    vmem = pl.BlockSpec(memory_space=pltpu.VMEM)
    return pl.pallas_call(
        functools.partial(tile_kernel, n_aux, own),
        grid=(count,),
        out_shape=(
            jax.ShapeDtypeStruct((n_aux, own, pairs), F32),
            jax.ShapeDtypeStruct((n_dev, own, pairs), BF16),
        ),
        in_specs=[smem] * 4 + [vmem] * 3 + [pl.BlockSpec((1, pairs, naux), lambda t: (t, 0, 0))],
        out_specs=(vmem, vmem),
        scratch_shapes=[pltpu.VMEM((n_dev, own, pairs), F32)],
        compiler_params=pltpu.CompilerParams(vmem_limit_bytes=48 * 1024 * 1024),
        name="tiles",
    )(sizes, rows, owners, blocks, occ, vir, adj, three)


def exchange_kernel(
    n_blk, n_aux, norm, sizes, occ_ref, vir_ref, occ_out, vir_out, occ_got, vir_got, occ_sems, vir_sems
):
    n_dev = n_blk * n_aux
    b = lax.axis_index("blk")
    a = lax.axis_index("aux")
    me = b * n_aux + a
    own, pairs = occ_out.shape
    barrier = pltpu.get_barrier_semaphore()

    def greet(k, carry):
        p = lax.rem(me + k, n_dev)
        pl.semaphore_signal(barrier, inc=1, device_id=(p // n_aux, p % n_aux), device_id_type=MESH)
        return carry

    lax.fori_loop(1, n_dev, greet, 0)
    pl.semaphore_wait(barrier, n_dev - 1)

    def vir_copy(k, source):
        p = lax.rem(me + k, n_dev)
        return pltpu.make_async_remote_copy(
            src_ref=vir_ref.at[p],
            dst_ref=vir_got.at[source],
            send_sem=vir_sems.at[0, k],
            recv_sem=vir_sems.at[1, source],
            device_id=(p // n_aux, p % n_aux),
            device_id_type=MESH,
        )

    def occ_copy(k, source):
        q = lax.rem(a + k, n_aux)
        return pltpu.make_async_remote_copy(
            src_ref=occ_ref.at[q],
            dst_ref=occ_got.at[source],
            send_sem=occ_sems.at[0, k],
            recv_sem=occ_sems.at[1, source],
            device_id=(b, q),
            device_id_type=MESH,
        )

    def start_vir(k, carry):
        vir_copy(k, me).start()
        return carry

    def start_occ(k, carry):
        occ_copy(k, a).start()
        return carry

    lax.fori_loop(1, n_dev, start_vir, 0)
    lax.fori_loop(1, n_aux, start_occ, 0)

    def take_vir(k, total):
        source = lax.rem(me + k, n_dev)
        vir_copy(k, source).wait_recv()
        return total + vir_got[source].astype(F32)

    def take_occ(k, total):
        source = lax.rem(a + k, n_aux)
        occ_copy(k, source).wait_recv()
        return total + occ_got[source]

    occ_sum = lax.fori_loop(1, n_aux, take_occ, occ_ref[a])
    vir_sum = lax.fori_loop(1, n_dev, take_vir, vir_ref[me].astype(F32))
    lane = iota((1, pairs), 1)
    for r in range(own):
        size = sizes[a * own + r]
        scale = jnp.where((lane // BS < size) & (lane % BS < size), norm, 0.0).astype(F32)
        occ_out[r : r + 1, :] = occ_sum[r : r + 1, :] * scale
        vir_out[r : r + 1, :] = vir_sum[r : r + 1, :] * scale

    def end_vir(k, carry):
        vir_copy(k, me).wait_send()
        return carry

    def end_occ(k, carry):
        occ_copy(k, a).wait_send()
        return carry

    lax.fori_loop(1, n_dev, end_vir, 0)
    lax.fori_loop(1, n_aux, end_occ, 0)


def exchange(sizes, occ, vir, n_blk, n_aux, norm):
    n_dev, own, pairs = vir.shape
    vmem = pl.BlockSpec(memory_space=pltpu.VMEM)
    out = jax.ShapeDtypeStruct((own, pairs), F32)
    return pl.pallas_call(
        functools.partial(exchange_kernel, n_blk, n_aux, norm),
        out_shape=(out, out),
        in_specs=[pl.BlockSpec(memory_space=pltpu.SMEM), vmem, vmem],
        out_specs=(vmem, vmem),
        scratch_shapes=[
            pltpu.VMEM(occ.shape, occ.dtype),
            pltpu.VMEM(vir.shape, vir.dtype),
            pltpu.SemaphoreType.DMA((2, n_aux)),
            pltpu.SemaphoreType.DMA((2, n_dev)),
        ],
        compiler_params=pltpu.CompilerParams(collective_id=1, has_side_effects=True),
        name="exchange",
    )(sizes, occ, vir)


def shards(
    n_blk, n_aux, adjoint, three_centre, occ_density, vir_density, block_sizes, tile_rows, col_owner, col_block
):
    n_dev = n_blk * n_aux
    count = three_centre.shape[0]
    naux = three_centre.shape[3]
    own = occ_density.shape[0] // n_aux
    depth = adjoint.shape[0]
    aux_here = lax.axis_index("aux")
    own_sizes = lax.dynamic_slice_in_dim(block_sizes, aux_here * own, own, 0)
    own_vir = lax.dynamic_slice_in_dim(vir_density, aux_here * own, own, 0)
    lane = jnp.arange(BS * BS, dtype=jnp.int32)[None, :]
    inside = (lane // BS < own_sizes[:, None]) & (lane % BS < own_sizes[:, None])
    own_vir = jnp.where(inside, own_vir, jnp.zeros_like(own_vir))
    got = gather(jnp.concatenate((adjoint, own_vir), axis=0), n_blk, n_aux)
    adj = got[:, :depth, :].reshape(naux, naux)
    vir = got[:, depth:, :]
    occ_terms, vir_terms = tiles(
        block_sizes, tile_rows, col_owner.reshape(count), col_block, occ_density, vir, adj,
        three_centre.reshape(count, BS * BS, naux), n_dev, n_aux,
    )
    return exchange(block_sizes, occ_terms, vir_terms, n_blk, n_aux, naux ** -0.5)


def solution(mesh):
    in_specs = (
        P(("blk", "aux"), None),
        P(("blk", "aux"), None, None, None),
        P("blk", None),
        P("blk", None),
        P("blk"),
        P(("blk", "aux")),
        P(("blk", "aux"), None),
        P(("blk", "aux")),
    )
    out_specs = (P(("blk", "aux"), None), P(("blk", "aux"), None))
    body = functools.partial(shards, mesh.shape["blk"], mesh.shape["aux"])
    return jax.shard_map(body, mesh=mesh, in_specs=in_specs, out_specs=out_specs, check_vma=False)
```

```python
import functools

import jax
import jax.numpy as jnp
from jax import lax
from jax.experimental import pallas as pl
from jax.experimental.pallas import tpu as pltpu
from jax.sharding import PartitionSpec as P

BS = 32
CHUNK = 256
MESH = pl.DeviceIdType.MESH
F32 = jnp.float32
BF16 = jnp.bfloat16


def iota(shape, dim):
    return lax.broadcasted_iota(jnp.int32, shape, dim)


def fold(minor, pairs):
    index = iota((pairs, 128), 0)
    index = index % BS if minor else index // BS
    return (index == iota((pairs, 128), 1) % BS).astype(BF16)


def dot(left, right):
    return jnp.dot(left, right, preferred_element_type=F32)


def dot_nt(left, right):
    return lax.dot_general(left, right, (((1,), (1,)), ((), ())), preferred_element_type=F32)


def fused_kernel(
    n_blk, n_aux, norm,
    sizes, rows, owners, blocks, adj_ref, occ_ref, vir_ref, t_hbm,
    occ_out, vir_out,
    got, tbuf, cbuf, occ_rep, vir_rep, occ_sums, vir_sums, occ_send, vir_send, occ_got, vir_got,
    t_sem, send_sem, recv_sem, occ_sems, vir_sems,
):
    n_dev = n_blk * n_aux
    depth = n_blk // 2
    count, pairs, naux = tbuf.shape
    own = occ_out.shape[0]
    arows = adj_ref.shape[0]
    span = naux // depth
    per_plane = n_dev // depth
    b = lax.axis_index("blk")
    a = lax.axis_index("aux")
    z, y, x, c = b // 2, b % 2, a // 2, a % 2
    up, down, over_x, over_y, mate = range(5)
    place = {
        up: (b + 2, a),
        down: (b - 2, a),
        over_x: (b, (1 - x) * 2 + c),
        over_y: (z * 2 + 1 - y, a),
        mate: (b, x * 2 + 1 - c),
    }
    has_up, has_down = z < depth - 1, z > 0
    me = b * n_aux + a

    def ident(xx, yy, zz, cc):
        return ((zz * 2 + yy) * 2 + xx) * 2 + cc

    barrier = pltpu.get_barrier_semaphore()

    def greet(k, carry):
        p = lax.rem(me + k, n_dev)
        pl.semaphore_signal(barrier, inc=1, device_id=(p // n_aux, p % n_aux), device_id_type=MESH)
        return carry

    lax.fori_loop(1, n_dev, greet, 0)
    fetches = [pltpu.make_async_copy(t_hbm.at[t], tbuf.at[t], t_sem.at[t]) for t in range(count)]
    for fetch in fetches:
        fetch.start()

    lane = iota((1, pairs), 1)
    major, minor = lane // BS, lane % BS
    got[me, :arows, :] = adj_ref[...]
    vir_all = vir_ref[...].astype(F32)
    slot = iota(vir_all.shape, 0)
    mine = []
    for r in range(own):
        size = sizes[a * own + r]
        row = jnp.sum(jnp.where(slot == a * own + r, vir_all, 0.0), axis=0, keepdims=True)
        mine.append(jnp.where((major < size) & (minor < size), row, 0.0))
    got[me, arows:, :] = jnp.concatenate(mine, axis=0).astype(BF16)

    diag = iota((BS, pairs), 1) // BS == iota((BS, pairs), 0)
    fold_minor = fold(True, pairs)
    pl.semaphore_wait(barrier, n_dev - 1)

    def copy(way, block):
        return pltpu.make_async_remote_copy(
            src_ref=got.at[block],
            dst_ref=got.at[block],
            send_sem=send_sem.at[way, block],
            recv_sem=recv_sem.at[block],
            device_id=place[way],
            device_id_type=MESH,
        )

    def send(way, block, when=None):
        if when is None:
            copy(way, block).start()
        else:

            @pl.when(when)
            def _():
                copy(way, block).start()

    def arrive(block):
        copy(mate, block).wait_recv()

    send(up, me, has_up)
    send(down, me, has_down)
    send(over_x, me)
    send(over_y, me)
    send(mate, me)

    occ_all = occ_ref[...].astype(F32)
    parts = []
    for t in range(count):
        size = sizes[rows[t]]
        row = jnp.sum(jnp.where(slot == rows[t], occ_all, 0.0), axis=0, keepdims=True)
        row = jnp.where((major < size) & (minor < size), row, 0.0)
        parts.append(jnp.where(diag, row, 0.0))
    spread = (iota((128, pairs), 0) == iota((128, pairs), 1) // BS).astype(BF16)
    square = dot(jnp.concatenate(parts, axis=0).astype(BF16), fold_minor)
    occ_rep[...] = dot(square.astype(BF16), spread).reshape(occ_rep.shape)

    def column(zz, from_up):
        block = ident(x, y, zz, c)
        arrive(block)
        if from_up:
            send(down, block, has_down)
        else:
            send(up, block, has_up)
        send(over_x, block)
        send(over_y, block)
        send(mate, block)

    def sides(zz, _):
        block = ident(1 - x, y, zz, c)
        arrive(block)
        send(over_y, block, zz % 2 == 0)
        send(mate, block)
        block = ident(x, 1 - y, zz, c)
        arrive(block)
        send(over_x, block, zz % 2 == 1)
        send(mate, block)

    def corner(zz, _):
        block = ident(1 - x, 1 - y, zz, c)
        arrive(block)
        send(mate, block)

    def mates(zz, _):
        for xx in (x, 1 - x):
            for yy in (y, 1 - y):
                arrive(ident(xx, yy, zz, 1 - c))

    def contract(zz, first, last):
        part = got[pl.ds(zz * per_plane, per_plane), :arows, :].reshape(span, naux)
        columns = pl.ds(pl.multiple_of(zz * span, span), span)

        def step(t, carry):
            cbuf[t, :, columns] = dot_nt(tbuf[t], part).astype(BF16)
            return carry

        lax.fori_loop(first, last, step, 0)

    def planes(dist, work):
        if dist == 0:
            work(z, None)
        elif dist < depth:

            @pl.when(z + dist < depth)
            def _():
                work(z + dist, True)

            @pl.when(z - dist >= 0)
            def _():
                work(z - dist, False)

    def whole(zz, _):
        mates(zz, _)
        contract(zz, 0, count)

    planes(1, column)
    planes(0, sides)
    planes(2, column)
    planes(1, sides)
    planes(0, corner)
    for fetch in fetches:
        fetch.wait()
    mates(z, None)
    contract(z, 0, count // 2)
    planes(3, column)
    planes(1, corner)
    planes(2, sides)
    contract(z, count // 2, count)
    for dist in range(1, depth):
        planes(dist + 3, column)
        planes(dist + 1, corner)
        planes(dist + 2, sides)
        planes(dist, whole)

    parts = []
    for t in range(count):
        home = owners[t] * n_aux + blocks[t] // own
        near = got[home, arows:, :].astype(F32)
        row = jnp.sum(jnp.where(iota(near.shape, 0) == blocks[t] % own, near, 0.0), axis=0, keepdims=True)
        parts.append(jnp.where(diag, row, 0.0))
    square = dot(jnp.concatenate(parts, axis=0).astype(BF16), fold_minor)
    vir_rep[...] = jnp.concatenate([square] * (pairs // 128), axis=1).reshape(vir_rep.shape)

    def tile(t, carry):
        acc = jnp.zeros((BS, pairs), F32)
        lines = []
        for first in range(0, pairs, CHUNK):
            gram = dot_nt(cbuf[t, first : first + CHUNK, :], tbuf[t])
            for at in range(CHUNK // BS):
                i = first // BS + at
                block_i = gram[at * BS : (at + 1) * BS, :]
                acc = acc + block_i * occ_rep[t, i : i + 1, :]
                lines.append(jnp.sum(block_i * vir_rep[t], axis=0, keepdims=True))
        vir_sums[t] = acc
        occ_sums[t] = jnp.concatenate(lines, axis=0)
        return carry

    lax.fori_loop(0, count, tile, 0)

    def flatten(mat, folding):
        high = mat.astype(BF16)
        low = (mat - high.astype(F32)).astype(BF16)
        both = dot(high, folding) + dot(low, folding)
        lines = []
        for t in range(count):
            wide = jnp.concatenate([both[t * BS : (t + 1) * BS]] * (pairs // 128), axis=1)
            lines.append(jnp.sum(jnp.where(diag, wide, 0.0), axis=0, keepdims=True))
        return lines

    vir_flat = flatten(vir_sums[...].reshape(count * BS, pairs), fold_minor)
    shape = (n_dev, own, 1)
    place_id = iota(shape, 0) * own + iota(shape, 1)
    total = jnp.zeros(vir_send.shape, F32)
    for t in range(count):
        hot = (place_id == owners[t] * (n_aux * own) + blocks[t]).astype(F32)
        total = total + hot * vir_flat[t].reshape(1, 1, pairs)
    vir_send[...] = total.astype(BF16)
    occ_flat = flatten(occ_sums[...].reshape(count * BS, pairs), fold(False, pairs))
    shape = (n_aux, own, 1)
    place_id = iota(shape, 0) * own + iota(shape, 1)
    total = jnp.zeros(occ_send.shape, F32)
    for t in range(count):
        hot = (place_id == rows[t]).astype(F32)
        total = total + hot * occ_flat[t].reshape(1, 1, pairs)
    occ_send[...] = total

    trade(
        n_blk, n_aux, norm, sizes, occ_send, vir_send, occ_out, vir_out, occ_got, vir_got, occ_sems, vir_sems
    )

    for zz in range(depth):
        block = ident(x, y, zz, c)
        for way in (over_x, over_y, mate):
            copy(way, block).wait_send()

        @pl.when((zz <= z) & has_up)
        def _():
            copy(up, ident(x, y, zz, c)).wait_send()

        @pl.when((zz >= z) & has_down)
        def _():
            copy(down, ident(x, y, zz, c)).wait_send()

        block = ident(1 - x, y, zz, c)
        copy(mate, block).wait_send()
        if zz % 2 == 0:
            copy(over_y, block).wait_send()
        block = ident(x, 1 - y, zz, c)
        copy(mate, block).wait_send()
        if zz % 2 == 1:
            copy(over_x, block).wait_send()
        copy(mate, ident(1 - x, 1 - y, zz, c)).wait_send()


def fused(sizes, rows, owners, blocks, adj, occ, vir, three, n_blk, n_aux, norm):
    n_dev = n_blk * n_aux
    count, pairs, naux = three.shape
    own = occ.shape[0] // n_aux
    smem = pl.BlockSpec(memory_space=pltpu.SMEM)
    vmem = pl.BlockSpec(memory_space=pltpu.VMEM)
    out = jax.ShapeDtypeStruct((own, pairs), F32)
    square = pltpu.VMEM((count, BS, pairs), F32)
    return pl.pallas_call(
        functools.partial(fused_kernel, n_blk, n_aux, norm),
        out_shape=(out, out),
        in_specs=[smem] * 4 + [vmem] * 3 + [pl.BlockSpec(memory_space=pl.ANY)],
        out_specs=(vmem, vmem),
        scratch_shapes=[
            pltpu.VMEM((n_dev, adj.shape[0] + own, naux), BF16),
            pltpu.VMEM((count, pairs, naux), BF16),
            pltpu.VMEM((count, pairs, naux), BF16),
            square,
            square,
            square,
            square,
            pltpu.VMEM((n_aux, own, pairs), F32),
            pltpu.VMEM((n_dev, own, pairs), BF16),
            pltpu.VMEM((n_aux, own, pairs), F32),
            pltpu.VMEM((n_dev, own, pairs), BF16),
            pltpu.SemaphoreType.DMA((count,)),
            pltpu.SemaphoreType.DMA((5, n_dev)),
            pltpu.SemaphoreType.DMA((n_dev,)),
            pltpu.SemaphoreType.DMA((2, n_aux)),
            pltpu.SemaphoreType.DMA((2, n_dev)),
        ],
        compiler_params=pltpu.CompilerParams(
            collective_id=0, has_side_effects=True, vmem_limit_bytes=50 * 1024 * 1024
        ),
        name="fused",
    )(sizes, rows, owners, blocks, adj, occ, vir, three)


def tile_kernel(
    n_aux, own, sizes, rows, owners, blocks, occ_ref, vir_ref, adj_ref, t_ref, occ_out, vir_out, vir_acc
):
    t = pl.program_id(0)
    pairs = BS * BS
    naux = adj_ref.shape[0]

    @pl.when(t == 0)
    def _():
        occ_out[...] = jnp.zeros_like(occ_out)
        vir_acc[...] = jnp.zeros_like(vir_acc)

    row, owner, block = rows[t], owners[t], blocks[t]
    size = sizes[row]
    lane = iota((1, pairs), 1)
    inside = (lane // BS < size) & (lane % BS < size)
    occ_all = occ_ref[...].astype(F32)
    occ_row = jnp.sum(jnp.where(iota(occ_all.shape, 0) == row, occ_all, 0.0), axis=0, keepdims=True)
    occ_row = jnp.where(inside, occ_row, 0.0)
    home = owner * n_aux + block // own
    vir_all = vir_ref[home].astype(F32)
    vir_row = jnp.sum(jnp.where(iota(vir_all.shape, 0) == block % own, vir_all, 0.0), axis=0, keepdims=True)
    diag = iota((BS, pairs), 1) // BS == iota((BS, pairs), 0)
    fold_minor = (iota((pairs, 128), 0) % BS == iota((pairs, 128), 1) % BS).astype(BF16)
    fold_major = (iota((pairs, 128), 0) // BS == iota((pairs, 128), 1) % BS).astype(BF16)
    spread = (iota((128, pairs), 0) == iota((128, pairs), 1) // BS).astype(BF16)
    repeat = pairs // 128

    def square(flat):
        return jnp.dot(jnp.where(diag, flat, 0.0).astype(BF16), fold_minor, preferred_element_type=F32)

    occ_rep = jnp.dot(square(occ_row).astype(BF16), spread, preferred_element_type=F32)
    vir_rep = jnp.concatenate([square(vir_row)] * repeat, axis=1)

    nt = (((1,), (1,)), ((), ()))
    acc = jnp.zeros((BS, pairs), F32)
    lines = []
    for first in range(0, pairs, CHUNK):
        part = lax.dot_general(t_ref[0, first : first + CHUNK, :], adj_ref[...], nt, preferred_element_type=F32)
        gram = lax.dot_general(part.astype(BF16), t_ref[0], nt, preferred_element_type=F32)
        for at in range(CHUNK // BS):
            i = first // BS + at
            block_i = gram[at * BS : (at + 1) * BS, :]
            acc = acc + block_i * occ_rep[i : i + 1, :]
            lines.append(jnp.sum(block_i * vir_rep, axis=0, keepdims=True))
    zmat = jnp.concatenate(lines, axis=0)

    def flatten(mat, fold):
        high = mat.astype(BF16)
        low = (mat - high.astype(F32)).astype(BF16)
        both = jnp.dot(high, fold, preferred_element_type=F32) + jnp.dot(low, fold, preferred_element_type=F32)
        wide = jnp.concatenate([both] * repeat, axis=1)
        return jnp.sum(jnp.where(diag, wide, 0.0), axis=0, keepdims=True)

    occ_flat = flatten(zmat, fold_major)
    vir_flat = flatten(acc, fold_minor)
    slot = iota((own, pairs), 0)
    occ_out[row // own] = occ_out[row // own] + jnp.where(slot == row % own, occ_flat, 0.0)
    vir_acc[home] = vir_acc[home] + jnp.where(slot == block % own, vir_flat, 0.0)

    @pl.when(t == pl.num_programs(0) - 1)
    def _():
        vir_out[...] = vir_acc[...].astype(vir_out.dtype)


def tiles(sizes, rows, owners, blocks, occ, vir, adj, three, n_dev, n_aux):
    count, pairs, naux = three.shape
    own = occ.shape[0] // n_aux
    smem = pl.BlockSpec(memory_space=pltpu.SMEM)
    vmem = pl.BlockSpec(memory_space=pltpu.VMEM)
    return pl.pallas_call(
        functools.partial(tile_kernel, n_aux, own),
        grid=(count,),
        out_shape=(
            jax.ShapeDtypeStruct((n_aux, own, pairs), F32),
            jax.ShapeDtypeStruct((n_dev, own, pairs), BF16),
        ),
        in_specs=[smem] * 4 + [vmem] * 3 + [pl.BlockSpec((1, pairs, naux), lambda t: (t, 0, 0))],
        out_specs=(vmem, vmem),
        scratch_shapes=[pltpu.VMEM((n_dev, own, pairs), F32)],
        compiler_params=pltpu.CompilerParams(vmem_limit_bytes=48 * 1024 * 1024),
        name="tiles",
    )(sizes, rows, owners, blocks, occ, vir, adj, three)


def exchange_kernel(
    n_blk, n_aux, norm, sizes, occ_ref, vir_ref, occ_out, vir_out, occ_got, vir_got, occ_sems, vir_sems
):
    n_dev = n_blk * n_aux
    b = lax.axis_index("blk")
    a = lax.axis_index("aux")
    me = b * n_aux + a
    barrier = pltpu.get_barrier_semaphore()

    def greet(k, carry):
        p = lax.rem(me + k, n_dev)
        pl.semaphore_signal(barrier, inc=1, device_id=(p // n_aux, p % n_aux), device_id_type=MESH)
        return carry

    lax.fori_loop(1, n_dev, greet, 0)
    pl.semaphore_wait(barrier, n_dev - 1)

    trade(n_blk, n_aux, norm, sizes, occ_ref, vir_ref, occ_out, vir_out, occ_got, vir_got, occ_sems, vir_sems)


def trade(n_blk, n_aux, norm, sizes, occ_ref, vir_ref, occ_out, vir_out, occ_got, vir_got, occ_sems, vir_sems):
    n_dev = n_blk * n_aux
    b = lax.axis_index("blk")
    a = lax.axis_index("aux")
    me = b * n_aux + a
    own, pairs = occ_out.shape

    def vir_copy(k, source):
        p = lax.rem(me + k, n_dev)
        return pltpu.make_async_remote_copy(
            src_ref=vir_ref.at[p],
            dst_ref=vir_got.at[source],
            send_sem=vir_sems.at[0, k],
            recv_sem=vir_sems.at[1, source],
            device_id=(p // n_aux, p % n_aux),
            device_id_type=MESH,
        )

    def occ_copy(k, source):
        q = lax.rem(a + k, n_aux)
        return pltpu.make_async_remote_copy(
            src_ref=occ_ref.at[q],
            dst_ref=occ_got.at[source],
            send_sem=occ_sems.at[0, k],
            recv_sem=occ_sems.at[1, source],
            device_id=(b, q),
            device_id_type=MESH,
        )

    def start_vir(k, carry):
        vir_copy(k, me).start()
        return carry

    def start_occ(k, carry):
        occ_copy(k, a).start()
        return carry

    lax.fori_loop(1, n_dev, start_vir, 0)
    lax.fori_loop(1, n_aux, start_occ, 0)

    def take_vir(k, total):
        source = lax.rem(me + k, n_dev)
        vir_copy(k, source).wait_recv()
        return total + vir_got[source].astype(F32)

    def take_occ(k, total):
        source = lax.rem(a + k, n_aux)
        occ_copy(k, source).wait_recv()
        return total + occ_got[source]

    occ_sum = lax.fori_loop(1, n_aux, take_occ, occ_ref[a])
    vir_sum = lax.fori_loop(1, n_dev, take_vir, vir_ref[me].astype(F32))
    lane = iota((1, pairs), 1)
    for r in range(own):
        size = sizes[a * own + r]
        scale = jnp.where((lane // BS < size) & (lane % BS < size), norm, 0.0).astype(F32)
        occ_out[r : r + 1, :] = occ_sum[r : r + 1, :] * scale
        vir_out[r : r + 1, :] = vir_sum[r : r + 1, :] * scale

    def end_vir(k, carry):
        vir_copy(k, me).wait_send()
        return carry

    def end_occ(k, carry):
        occ_copy(k, a).wait_send()
        return carry

    lax.fori_loop(1, n_dev, end_vir, 0)
    lax.fori_loop(1, n_aux, end_occ, 0)


def exchange(sizes, occ, vir, n_blk, n_aux, norm):
    n_dev, own, pairs = vir.shape
    vmem = pl.BlockSpec(memory_space=pltpu.VMEM)
    out = jax.ShapeDtypeStruct((own, pairs), F32)
    return pl.pallas_call(
        functools.partial(exchange_kernel, n_blk, n_aux, norm),
        out_shape=(out, out),
        in_specs=[pl.BlockSpec(memory_space=pltpu.SMEM), vmem, vmem],
        out_specs=(vmem, vmem),
        scratch_shapes=[
            pltpu.VMEM(occ.shape, occ.dtype),
            pltpu.VMEM(vir.shape, vir.dtype),
            pltpu.SemaphoreType.DMA((2, n_aux)),
            pltpu.SemaphoreType.DMA((2, n_dev)),
        ],
        compiler_params=pltpu.CompilerParams(collective_id=1, has_side_effects=True),
        name="exchange",
    )(sizes, occ, vir)


def shards(
    n_blk, n_aux, adjoint, three_centre, occ_density, vir_density, block_sizes, tile_rows, col_owner, col_block
):
    n_dev = n_blk * n_aux
    count = three_centre.shape[0]
    naux = three_centre.shape[3]
    own = occ_density.shape[0] // n_aux
    depth = adjoint.shape[0]
    three = three_centre.reshape(count, BS * BS, naux)
    if n_aux == 4 and n_blk % 2 == 0:
        return fused(
            block_sizes, tile_rows, col_owner.reshape(count), col_block, adjoint, occ_density, vir_density,
            three, n_blk, n_aux, naux ** -0.5,
        )
    aux_here = lax.axis_index("aux")
    own_sizes = lax.dynamic_slice_in_dim(block_sizes, aux_here * own, own, 0)
    own_vir = lax.dynamic_slice_in_dim(vir_density, aux_here * own, own, 0)
    lane = jnp.arange(BS * BS, dtype=jnp.int32)[None, :]
    inside = (lane // BS < own_sizes[:, None]) & (lane % BS < own_sizes[:, None])
    own_vir = jnp.where(inside, own_vir, jnp.zeros_like(own_vir))
    got = lax.all_gather(jnp.concatenate((adjoint, own_vir), axis=0), ("blk", "aux"), axis=0)
    adj = got[:, :depth, :].reshape(naux, naux)
    vir = got[:, depth:, :]
    occ_terms, vir_terms = tiles(
        block_sizes, tile_rows, col_owner.reshape(count), col_block, occ_density, vir, adj,
        three, n_dev, n_aux,
    )
    return exchange(block_sizes, occ_terms, vir_terms, n_blk, n_aux, naux ** -0.5)


def solution(mesh):
    in_specs = (
        P(("blk", "aux"), None),
        P(("blk", "aux"), None, None, None),
        P("blk", None),
        P("blk", None),
        P("blk"),
        P(("blk", "aux")),
        P(("blk", "aux"), None),
        P(("blk", "aux")),
    )
    out_specs = (P(("blk", "aux"), None), P(("blk", "aux"), None))
    body = functools.partial(shards, mesh.shape["blk"], mesh.shape["aux"])
    return jax.shard_map(body, mesh=mesh, in_specs=in_specs, out_specs=out_specs, check_vma=False)
```

```python
import functools

import jax
import jax.numpy as jnp
from jax import lax
from jax.experimental import pallas as pl
from jax.experimental.pallas import tpu as pltpu
from jax.sharding import PartitionSpec as P

BS = 32
CHUNK = 256
MESH = pl.DeviceIdType.MESH
F32 = jnp.float32
BF16 = jnp.bfloat16


def iota(shape, dim):
    return lax.broadcasted_iota(jnp.int32, shape, dim)


def fold(minor, pairs):
    index = iota((pairs, 128), 0)
    index = index % BS if minor else index // BS
    return (index == iota((pairs, 128), 1) % BS).astype(BF16)


def dot(left, right):
    return jnp.dot(left, right, preferred_element_type=F32)


def dot_nt(left, right):
    return lax.dot_general(left, right, (((1,), (1,)), ((), ())), preferred_element_type=F32)


def fused_kernel(
    n_blk, n_aux, norm,
    sizes, rows, owners, blocks, adj_ref, occ_ref, vir_ref, t_hbm,
    occ_out, vir_out,
    got, tbuf, cbuf, occ_rep, vir_rep, occ_sums, vir_sums, occ_send, vir_send, occ_got, vir_got,
    t_sem, send_sem, recv_sem, occ_sems, vir_sems,
):
    n_dev = n_blk * n_aux
    depth = n_blk // 2
    count, pairs, naux = tbuf.shape
    own = occ_out.shape[0]
    arows = adj_ref.shape[0]
    span = naux // depth
    per_plane = n_dev // depth
    b = lax.axis_index("blk")
    a = lax.axis_index("aux")
    z, y, x, c = b // 2, b % 2, a // 2, a % 2
    up, down, over_x, over_y, mate = range(5)
    place = {
        up: (b + 2, a),
        down: (b - 2, a),
        over_x: (b, (1 - x) * 2 + c),
        over_y: (z * 2 + 1 - y, a),
        mate: (b, x * 2 + 1 - c),
    }
    has_up, has_down = z < depth - 1, z > 0
    me = b * n_aux + a

    def ident(xx, yy, zz, cc):
        return ((zz * 2 + yy) * 2 + xx) * 2 + cc

    barrier = pltpu.get_barrier_semaphore()

    def greet(k, carry):
        p = lax.rem(me + k, n_dev)
        pl.semaphore_signal(barrier, inc=1, device_id=(p // n_aux, p % n_aux), device_id_type=MESH)
        return carry

    lax.fori_loop(1, n_dev, greet, 0)
    fetches = [pltpu.make_async_copy(t_hbm.at[t], tbuf.at[t], t_sem.at[t]) for t in range(count)]
    for fetch in fetches:
        fetch.start()

    lane = iota((1, pairs), 1)
    major, minor = lane // BS, lane % BS
    got[me, :arows, :] = adj_ref[...]
    vir_all = vir_ref[...].astype(F32)
    slot = iota(vir_all.shape, 0)
    mine = []
    for r in range(own):
        size = sizes[a * own + r]
        row = jnp.sum(jnp.where(slot == a * own + r, vir_all, 0.0), axis=0, keepdims=True)
        mine.append(jnp.where((major < size) & (minor < size), row, 0.0))
    got[me, arows:, :] = jnp.concatenate(mine, axis=0).astype(BF16)

    diag = iota((BS, pairs), 1) // BS == iota((BS, pairs), 0)
    fold_minor = fold(True, pairs)
    pl.semaphore_wait(barrier, n_dev - 1)

    def copy(way, block):
        return pltpu.make_async_remote_copy(
            src_ref=got.at[block],
            dst_ref=got.at[block],
            send_sem=send_sem.at[way, block],
            recv_sem=recv_sem.at[block],
            device_id=place[way],
            device_id_type=MESH,
        )

    def send(way, block, when=None):
        if when is None:
            copy(way, block).start()
        else:

            @pl.when(when)
            def _():
                copy(way, block).start()

    def arrive(block):
        copy(mate, block).wait_recv()

    send(up, me, has_up)
    send(down, me, has_down)
    send(over_x, me)
    send(over_y, me)
    send(mate, me)

    occ_all = occ_ref[...].astype(F32)
    parts = []
    for t in range(count):
        size = sizes[rows[t]]
        row = jnp.sum(jnp.where(slot == rows[t], occ_all, 0.0), axis=0, keepdims=True)
        row = jnp.where((major < size) & (minor < size), row, 0.0)
        parts.append(jnp.where(diag, row, 0.0))
    spread = (iota((128, pairs), 0) == iota((128, pairs), 1) // BS).astype(BF16)
    square = dot(jnp.concatenate(parts, axis=0).astype(BF16), fold_minor)
    occ_rep[...] = dot(square.astype(BF16), spread).reshape(occ_rep.shape)

    def column(zz, from_up):
        block = ident(x, y, zz, c)
        arrive(block)
        if from_up:
            send(down, block, has_down)
        else:
            send(up, block, has_up)
        send(over_x, block)
        send(over_y, block)
        send(mate, block)

    def sides(zz, _):
        block = ident(1 - x, y, zz, c)
        arrive(block)
        send(over_y, block, zz % 2 == 0)
        send(mate, block)
        block = ident(x, 1 - y, zz, c)
        arrive(block)
        send(over_x, block, zz % 2 == 1)
        send(mate, block)

    def corner(zz, _):
        block = ident(1 - x, 1 - y, zz, c)
        arrive(block)
        send(mate, block)

    def mates(zz, _):
        for xx in (x, 1 - x):
            for yy in (y, 1 - y):
                arrive(ident(xx, yy, zz, 1 - c))

    def contract(zz, first, last):
        part = got[pl.ds(zz * per_plane, per_plane), :arows, :].reshape(span, naux)
        columns = pl.ds(pl.multiple_of(zz * span, span), span)

        def step(t, carry):
            cbuf[t, :, columns] = dot_nt(tbuf[t], part).astype(BF16)
            return carry

        lax.fori_loop(first, last, step, 0)

    def planes(dist, work):
        if dist == 0:
            work(z, None)
        elif dist < depth:

            @pl.when(z + dist < depth)
            def _():
                work(z + dist, True)

            @pl.when(z - dist >= 0)
            def _():
                work(z - dist, False)

    def whole(zz, _):
        mates(zz, _)
        contract(zz, 0, count)

    planes(1, column)
    planes(0, sides)
    planes(2, column)
    planes(1, sides)
    planes(0, corner)
    for fetch in fetches:
        fetch.wait()
    mates(z, None)
    contract(z, 0, count // 2)
    planes(3, column)
    contract(z, count // 2, count)
    for dist in range(1, depth):
        planes(dist, corner)
        planes(dist + 1, sides)
        planes(dist, whole)
        planes(dist + 3, column)

    parts = []
    for t in range(count):
        home = owners[t] * n_aux + blocks[t] // own
        near = got[home, arows:, :].astype(F32)
        row = jnp.sum(jnp.where(iota(near.shape, 0) == blocks[t] % own, near, 0.0), axis=0, keepdims=True)
        parts.append(jnp.where(diag, row, 0.0))
    square = dot(jnp.concatenate(parts, axis=0).astype(BF16), fold_minor)
    vir_rep[...] = jnp.concatenate([square] * (pairs // 128), axis=1).reshape(vir_rep.shape)

    def tile(t, carry):
        acc = jnp.zeros((BS, pairs), F32)
        lines = []
        for first in range(0, pairs, CHUNK):
            gram = dot_nt(cbuf[t, first : first + CHUNK, :], tbuf[t])
            for at in range(CHUNK // BS):
                i = first // BS + at
                block_i = gram[at * BS : (at + 1) * BS, :]
                acc = acc + block_i * occ_rep[t, i : i + 1, :]
                lines.append(jnp.sum(block_i * vir_rep[t], axis=0, keepdims=True))
        vir_sums[t] = acc
        occ_sums[t] = jnp.concatenate(lines, axis=0)
        return carry

    lax.fori_loop(0, count, tile, 0)

    def flatten(mat, folding):
        high = mat.astype(BF16)
        low = (mat - high.astype(F32)).astype(BF16)
        both = dot(high, folding) + dot(low, folding)
        lines = []
        for t in range(count):
            wide = jnp.concatenate([both[t * BS : (t + 1) * BS]] * (pairs // 128), axis=1)
            lines.append(jnp.sum(jnp.where(diag, wide, 0.0), axis=0, keepdims=True))
        return lines

    vir_flat = flatten(vir_sums[...].reshape(count * BS, pairs), fold_minor)
    shape = (n_dev, own, 1)
    place_id = iota(shape, 0) * own + iota(shape, 1)
    total = jnp.zeros(vir_send.shape, F32)
    for t in range(count):
        hot = (place_id == owners[t] * (n_aux * own) + blocks[t]).astype(F32)
        total = total + hot * vir_flat[t].reshape(1, 1, pairs)
    vir_send[...] = total.astype(BF16)
    occ_flat = flatten(occ_sums[...].reshape(count * BS, pairs), fold(False, pairs))
    shape = (n_aux, own, 1)
    place_id = iota(shape, 0) * own + iota(shape, 1)
    total = jnp.zeros(occ_send.shape, F32)
    for t in range(count):
        hot = (place_id == rows[t]).astype(F32)
        total = total + hot * occ_flat[t].reshape(1, 1, pairs)
    occ_send[...] = total

    trade(
        n_blk, n_aux, norm, sizes, occ_send, vir_send, occ_out, vir_out, occ_got, vir_got, occ_sems, vir_sems
    )

    for zz in range(depth):
        block = ident(x, y, zz, c)
        for way in (over_x, over_y, mate):
            copy(way, block).wait_send()

        @pl.when((zz <= z) & has_up)
        def _():
            copy(up, ident(x, y, zz, c)).wait_send()

        @pl.when((zz >= z) & has_down)
        def _():
            copy(down, ident(x, y, zz, c)).wait_send()

        block = ident(1 - x, y, zz, c)
        copy(mate, block).wait_send()
        if zz % 2 == 0:
            copy(over_y, block).wait_send()
        block = ident(x, 1 - y, zz, c)
        copy(mate, block).wait_send()
        if zz % 2 == 1:
            copy(over_x, block).wait_send()
        copy(mate, ident(1 - x, 1 - y, zz, c)).wait_send()


def fused(sizes, rows, owners, blocks, adj, occ, vir, three, n_blk, n_aux, norm):
    n_dev = n_blk * n_aux
    count, pairs, naux = three.shape
    own = occ.shape[0] // n_aux
    smem = pl.BlockSpec(memory_space=pltpu.SMEM)
    vmem = pl.BlockSpec(memory_space=pltpu.VMEM)
    out = jax.ShapeDtypeStruct((own, pairs), F32)
    square = pltpu.VMEM((count, BS, pairs), F32)
    return pl.pallas_call(
        functools.partial(fused_kernel, n_blk, n_aux, norm),
        out_shape=(out, out),
        in_specs=[smem] * 4 + [vmem] * 3 + [pl.BlockSpec(memory_space=pl.ANY)],
        out_specs=(vmem, vmem),
        scratch_shapes=[
            pltpu.VMEM((n_dev, adj.shape[0] + own, naux), BF16),
            pltpu.VMEM((count, pairs, naux), BF16),
            pltpu.VMEM((count, pairs, naux), BF16),
            square,
            square,
            square,
            square,
            pltpu.VMEM((n_aux, own, pairs), F32),
            pltpu.VMEM((n_dev, own, pairs), BF16),
            pltpu.VMEM((n_aux, own, pairs), F32),
            pltpu.VMEM((n_dev, own, pairs), BF16),
            pltpu.SemaphoreType.DMA((count,)),
            pltpu.SemaphoreType.DMA((5, n_dev)),
            pltpu.SemaphoreType.DMA((n_dev,)),
            pltpu.SemaphoreType.DMA((2, n_aux)),
            pltpu.SemaphoreType.DMA((2, n_dev)),
        ],
        compiler_params=pltpu.CompilerParams(
            collective_id=0, has_side_effects=True, vmem_limit_bytes=67043328
        ),
        name="fused",
    )(sizes, rows, owners, blocks, adj, occ, vir, three)


def tile_kernel(
    n_aux, own, sizes, rows, owners, blocks, occ_ref, vir_ref, adj_ref, t_ref, occ_out, vir_out, vir_acc
):
    t = pl.program_id(0)
    pairs = BS * BS
    naux = adj_ref.shape[0]

    @pl.when(t == 0)
    def _():
        occ_out[...] = jnp.zeros_like(occ_out)
        vir_acc[...] = jnp.zeros_like(vir_acc)

    row, owner, block = rows[t], owners[t], blocks[t]
    size = sizes[row]
    lane = iota((1, pairs), 1)
    inside = (lane // BS < size) & (lane % BS < size)
    occ_all = occ_ref[...].astype(F32)
    occ_row = jnp.sum(jnp.where(iota(occ_all.shape, 0) == row, occ_all, 0.0), axis=0, keepdims=True)
    occ_row = jnp.where(inside, occ_row, 0.0)
    home = owner * n_aux + block // own
    vir_all = vir_ref[home].astype(F32)
    vir_row = jnp.sum(jnp.where(iota(vir_all.shape, 0) == block % own, vir_all, 0.0), axis=0, keepdims=True)
    diag = iota((BS, pairs), 1) // BS == iota((BS, pairs), 0)
    fold_minor = (iota((pairs, 128), 0) % BS == iota((pairs, 128), 1) % BS).astype(BF16)
    fold_major = (iota((pairs, 128), 0) // BS == iota((pairs, 128), 1) % BS).astype(BF16)
    spread = (iota((128, pairs), 0) == iota((128, pairs), 1) // BS).astype(BF16)
    repeat = pairs // 128

    def square(flat):
        return jnp.dot(jnp.where(diag, flat, 0.0).astype(BF16), fold_minor, preferred_element_type=F32)

    occ_rep = jnp.dot(square(occ_row).astype(BF16), spread, preferred_element_type=F32)
    vir_rep = jnp.concatenate([square(vir_row)] * repeat, axis=1)

    nt = (((1,), (1,)), ((), ()))
    acc = jnp.zeros((BS, pairs), F32)
    lines = []
    for first in range(0, pairs, CHUNK):
        part = lax.dot_general(t_ref[0, first : first + CHUNK, :], adj_ref[...], nt, preferred_element_type=F32)
        gram = lax.dot_general(part.astype(BF16), t_ref[0], nt, preferred_element_type=F32)
        for at in range(CHUNK // BS):
            i = first // BS + at
            block_i = gram[at * BS : (at + 1) * BS, :]
            acc = acc + block_i * occ_rep[i : i + 1, :]
            lines.append(jnp.sum(block_i * vir_rep, axis=0, keepdims=True))
    zmat = jnp.concatenate(lines, axis=0)

    def flatten(mat, fold):
        high = mat.astype(BF16)
        low = (mat - high.astype(F32)).astype(BF16)
        both = jnp.dot(high, fold, preferred_element_type=F32) + jnp.dot(low, fold, preferred_element_type=F32)
        wide = jnp.concatenate([both] * repeat, axis=1)
        return jnp.sum(jnp.where(diag, wide, 0.0), axis=0, keepdims=True)

    occ_flat = flatten(zmat, fold_major)
    vir_flat = flatten(acc, fold_minor)
    slot = iota((own, pairs), 0)
    occ_out[row // own] = occ_out[row // own] + jnp.where(slot == row % own, occ_flat, 0.0)
    vir_acc[home] = vir_acc[home] + jnp.where(slot == block % own, vir_flat, 0.0)

    @pl.when(t == pl.num_programs(0) - 1)
    def _():
        vir_out[...] = vir_acc[...].astype(vir_out.dtype)


def tiles(sizes, rows, owners, blocks, occ, vir, adj, three, n_dev, n_aux):
    count, pairs, naux = three.shape
    own = occ.shape[0] // n_aux
    smem = pl.BlockSpec(memory_space=pltpu.SMEM)
    vmem = pl.BlockSpec(memory_space=pltpu.VMEM)
    return pl.pallas_call(
        functools.partial(tile_kernel, n_aux, own),
        grid=(count,),
        out_shape=(
            jax.ShapeDtypeStruct((n_aux, own, pairs), F32),
            jax.ShapeDtypeStruct((n_dev, own, pairs), BF16),
        ),
        in_specs=[smem] * 4 + [vmem] * 3 + [pl.BlockSpec((1, pairs, naux), lambda t: (t, 0, 0))],
        out_specs=(vmem, vmem),
        scratch_shapes=[pltpu.VMEM((n_dev, own, pairs), F32)],
        compiler_params=pltpu.CompilerParams(vmem_limit_bytes=48 * 1024 * 1024),
        name="tiles",
    )(sizes, rows, owners, blocks, occ, vir, adj, three)


def exchange_kernel(
    n_blk, n_aux, norm, sizes, occ_ref, vir_ref, occ_out, vir_out, occ_got, vir_got, occ_sems, vir_sems
):
    n_dev = n_blk * n_aux
    b = lax.axis_index("blk")
    a = lax.axis_index("aux")
    me = b * n_aux + a
    barrier = pltpu.get_barrier_semaphore()

    def greet(k, carry):
        p = lax.rem(me + k, n_dev)
        pl.semaphore_signal(barrier, inc=1, device_id=(p // n_aux, p % n_aux), device_id_type=MESH)
        return carry

    lax.fori_loop(1, n_dev, greet, 0)
    pl.semaphore_wait(barrier, n_dev - 1)

    trade(n_blk, n_aux, norm, sizes, occ_ref, vir_ref, occ_out, vir_out, occ_got, vir_got, occ_sems, vir_sems)


def trade(n_blk, n_aux, norm, sizes, occ_ref, vir_ref, occ_out, vir_out, occ_got, vir_got, occ_sems, vir_sems):
    n_dev = n_blk * n_aux
    b = lax.axis_index("blk")
    a = lax.axis_index("aux")
    me = b * n_aux + a
    own, pairs = occ_out.shape

    def vir_copy(k, source):
        p = lax.rem(me + k, n_dev)
        return pltpu.make_async_remote_copy(
            src_ref=vir_ref.at[p],
            dst_ref=vir_got.at[source],
            send_sem=vir_sems.at[0, k],
            recv_sem=vir_sems.at[1, source],
            device_id=(p // n_aux, p % n_aux),
            device_id_type=MESH,
        )

    def occ_copy(k, source):
        q = lax.rem(a + k, n_aux)
        return pltpu.make_async_remote_copy(
            src_ref=occ_ref.at[q],
            dst_ref=occ_got.at[source],
            send_sem=occ_sems.at[0, k],
            recv_sem=occ_sems.at[1, source],
            device_id=(b, q),
            device_id_type=MESH,
        )

    def start_vir(k, carry):
        vir_copy(k, me).start()
        return carry

    def start_occ(k, carry):
        occ_copy(k, a).start()
        return carry

    lax.fori_loop(1, n_dev, start_vir, 0)
    lax.fori_loop(1, n_aux, start_occ, 0)

    def take_vir(k, total):
        source = lax.rem(me + k, n_dev)
        vir_copy(k, source).wait_recv()
        return total + vir_got[source].astype(F32)

    def take_occ(k, total):
        source = lax.rem(a + k, n_aux)
        occ_copy(k, source).wait_recv()
        return total + occ_got[source]

    occ_sum = lax.fori_loop(1, n_aux, take_occ, occ_ref[a])
    vir_sum = lax.fori_loop(1, n_dev, take_vir, vir_ref[me].astype(F32))
    lane = iota((1, pairs), 1)
    for r in range(own):
        size = sizes[a * own + r]
        scale = jnp.where((lane // BS < size) & (lane % BS < size), norm, 0.0).astype(F32)
        occ_out[r : r + 1, :] = occ_sum[r : r + 1, :] * scale
        vir_out[r : r + 1, :] = vir_sum[r : r + 1, :] * scale

    def end_vir(k, carry):
        vir_copy(k, me).wait_send()
        return carry

    def end_occ(k, carry):
        occ_copy(k, a).wait_send()
        return carry

    lax.fori_loop(1, n_dev, end_vir, 0)
    lax.fori_loop(1, n_aux, end_occ, 0)


def exchange(sizes, occ, vir, n_blk, n_aux, norm):
    n_dev, own, pairs = vir.shape
    vmem = pl.BlockSpec(memory_space=pltpu.VMEM)
    out = jax.ShapeDtypeStruct((own, pairs), F32)
    return pl.pallas_call(
        functools.partial(exchange_kernel, n_blk, n_aux, norm),
        out_shape=(out, out),
        in_specs=[pl.BlockSpec(memory_space=pltpu.SMEM), vmem, vmem],
        out_specs=(vmem, vmem),
        scratch_shapes=[
            pltpu.VMEM(occ.shape, occ.dtype),
            pltpu.VMEM(vir.shape, vir.dtype),
            pltpu.SemaphoreType.DMA((2, n_aux)),
            pltpu.SemaphoreType.DMA((2, n_dev)),
        ],
        compiler_params=pltpu.CompilerParams(collective_id=1, has_side_effects=True),
        name="exchange",
    )(sizes, occ, vir)


def shards(
    n_blk, n_aux, adjoint, three_centre, occ_density, vir_density, block_sizes, tile_rows, col_owner, col_block
):
    n_dev = n_blk * n_aux
    count = three_centre.shape[0]
    naux = three_centre.shape[3]
    own = occ_density.shape[0] // n_aux
    depth = adjoint.shape[0]
    three = three_centre.reshape(count, BS * BS, naux)
    if n_aux == 4 and n_blk % 2 == 0:
        return fused(
            block_sizes, tile_rows, col_owner.reshape(count), col_block, adjoint, occ_density, vir_density,
            three, n_blk, n_aux, naux ** -0.5,
        )
    aux_here = lax.axis_index("aux")
    own_sizes = lax.dynamic_slice_in_dim(block_sizes, aux_here * own, own, 0)
    own_vir = lax.dynamic_slice_in_dim(vir_density, aux_here * own, own, 0)
    lane = jnp.arange(BS * BS, dtype=jnp.int32)[None, :]
    inside = (lane // BS < own_sizes[:, None]) & (lane % BS < own_sizes[:, None])
    own_vir = jnp.where(inside, own_vir, jnp.zeros_like(own_vir))
    got = lax.all_gather(jnp.concatenate((adjoint, own_vir), axis=0), ("blk", "aux"), axis=0)
    adj = got[:, :depth, :].reshape(naux, naux)
    vir = got[:, depth:, :]
    occ_terms, vir_terms = tiles(
        block_sizes, tile_rows, col_owner.reshape(count), col_block, occ_density, vir, adj,
        three, n_dev, n_aux,
    )
    return exchange(block_sizes, occ_terms, vir_terms, n_blk, n_aux, naux ** -0.5)


def solution(mesh):
    in_specs = (
        P(("blk", "aux"), None),
        P(("blk", "aux"), None, None, None),
        P("blk", None),
        P("blk", None),
        P("blk"),
        P(("blk", "aux")),
        P(("blk", "aux"), None),
        P(("blk", "aux")),
    )
    out_specs = (P(("blk", "aux"), None), P(("blk", "aux"), None))
    body = functools.partial(shards, mesh.shape["blk"], mesh.shape["aux"])
    return jax.shard_map(body, mesh=mesh, in_specs=in_specs, out_specs=out_specs, check_vma=False)
```

```python
import functools

import jax
import jax.numpy as jnp
from jax import lax
from jax.experimental import pallas as pl
from jax.experimental.pallas import tpu as pltpu
from jax.sharding import PartitionSpec as P

BS = 32
CHUNK = 256
MESH = pl.DeviceIdType.MESH
F32 = jnp.float32
BF16 = jnp.bfloat16


def iota(shape, dim):
    return lax.broadcasted_iota(jnp.int32, shape, dim)


def fold(minor, pairs):
    index = iota((pairs, 128), 0)
    index = index % BS if minor else index // BS
    return (index == iota((pairs, 128), 1) % BS).astype(BF16)


def dot(left, right):
    return jnp.dot(left, right, preferred_element_type=F32)


def dot_nt(left, right):
    return lax.dot_general(left, right, (((1,), (1,)), ((), ())), preferred_element_type=F32)


def fused_kernel(
    n_blk, n_aux, norm,
    sizes, rows, owners, blocks, adj_ref, occ_ref, vir_ref, t_hbm,
    out_ref,
    got, tbuf, cbuf, occ_rep, vir_rep, occ_sums, vir_sums, occ_send, vir_send, occ_got, vir_got,
    t_sem, send_sem, recv_sem, occ_sems, vir_sems,
):
    n_dev = n_blk * n_aux
    occ_out, vir_out = out_ref.at[0], out_ref.at[1]
    depth = n_blk // 2
    count, pairs, naux = tbuf.shape
    own = occ_out.shape[0]
    arows = adj_ref.shape[0]
    span = naux // depth
    per_plane = n_dev // depth
    b = lax.axis_index("blk")
    a = lax.axis_index("aux")
    z, y, x, c = b // 2, b % 2, a // 2, a % 2
    up, down, over_x, over_y, mate = range(5)
    place = {
        up: (b + 2, a),
        down: (b - 2, a),
        over_x: (b, (1 - x) * 2 + c),
        over_y: (z * 2 + 1 - y, a),
        mate: (b, x * 2 + 1 - c),
    }
    has_up, has_down = z < depth - 1, z > 0
    me = b * n_aux + a

    def ident(xx, yy, zz, cc):
        return ((zz * 2 + yy) * 2 + xx) * 2 + cc

    barrier = pltpu.get_barrier_semaphore()

    def greet(k, carry):
        p = lax.rem(me + k, n_dev)
        pl.semaphore_signal(barrier, inc=1, device_id=(p // n_aux, p % n_aux), device_id_type=MESH)
        return carry

    lax.fori_loop(1, n_dev, greet, 0)
    fetches = [pltpu.make_async_copy(t_hbm.at[t], tbuf.at[t], t_sem.at[t]) for t in range(count)]
    for fetch in fetches:
        fetch.start()

    lane = iota((1, pairs), 1)
    major, minor = lane // BS, lane % BS
    got[me, :arows, :] = adj_ref[...]
    vir_all = vir_ref[...].astype(F32)
    slot = iota(vir_all.shape, 0)
    mine = []
    for r in range(own):
        size = sizes[a * own + r]
        row = jnp.sum(jnp.where(slot == a * own + r, vir_all, 0.0), axis=0, keepdims=True)
        mine.append(jnp.where((major < size) & (minor < size), row, 0.0))
    got[me, arows:, :] = jnp.concatenate(mine, axis=0).astype(BF16)

    diag = iota((BS, pairs), 1) // BS == iota((BS, pairs), 0)
    fold_minor = fold(True, pairs)
    pl.semaphore_wait(barrier, n_dev - 1)

    def copy(way, block):
        return pltpu.make_async_remote_copy(
            src_ref=got.at[block],
            dst_ref=got.at[block],
            send_sem=send_sem.at[way, block],
            recv_sem=recv_sem.at[block],
            device_id=place[way],
            device_id_type=MESH,
        )

    def send(way, block, when=None):
        if when is None:
            copy(way, block).start()
        else:

            @pl.when(when)
            def _():
                copy(way, block).start()

    def arrive(block):
        copy(mate, block).wait_recv()

    send(up, me, has_up)
    send(down, me, has_down)
    send(over_x, me)
    send(over_y, me)
    send(mate, me)

    occ_all = occ_ref[...].astype(F32)
    parts = []
    for t in range(count):
        size = sizes[rows[t]]
        row = jnp.sum(jnp.where(slot == rows[t], occ_all, 0.0), axis=0, keepdims=True)
        row = jnp.where((major < size) & (minor < size), row, 0.0)
        parts.append(jnp.where(diag, row, 0.0))
    spread = (iota((128, pairs), 0) == iota((128, pairs), 1) // BS).astype(BF16)
    square = dot(jnp.concatenate(parts, axis=0).astype(BF16), fold_minor)
    occ_rep[...] = dot(square.astype(BF16), spread).reshape(occ_rep.shape)

    def column(zz, from_up):
        block = ident(x, y, zz, c)
        arrive(block)
        if from_up:
            send(down, block, has_down)
        else:
            send(up, block, has_up)
        send(over_x, block)
        send(over_y, block)
        send(mate, block)

    def sides(zz, _):
        block = ident(1 - x, y, zz, c)
        arrive(block)
        send(over_y, block, zz % 2 == 0)
        send(mate, block)
        block = ident(x, 1 - y, zz, c)
        arrive(block)
        send(over_x, block, zz % 2 == 1)
        send(mate, block)

    def corner(zz, _):
        block = ident(1 - x, 1 - y, zz, c)
        arrive(block)
        send(mate, block)

    def mates(zz, _):
        for xx in (x, 1 - x):
            for yy in (y, 1 - y):
                arrive(ident(xx, yy, zz, 1 - c))

    def contract(zz, first, last):
        part = got[pl.ds(zz * per_plane, per_plane), :arows, :].reshape(span, naux)
        columns = pl.ds(pl.multiple_of(zz * span, span), span)

        def step(t, carry):
            cbuf[t, :, columns] = dot_nt(tbuf[t], part).astype(BF16)
            return carry

        lax.fori_loop(first, last, step, 0)

    def planes(dist, work):
        if dist == 0:
            work(z, None)
        elif dist < depth:

            @pl.when(z + dist < depth)
            def _():
                work(z + dist, True)

            @pl.when(z - dist >= 0)
            def _():
                work(z - dist, False)

    def whole(zz, _):
        mates(zz, _)
        contract(zz, 0, count)

    planes(1, column)
    planes(0, sides)
    planes(2, column)
    planes(1, sides)
    planes(0, corner)
    for fetch in fetches:
        fetch.wait()
    mates(z, None)
    contract(z, 0, count // 2)
    planes(3, column)
    contract(z, count // 2, count)
    for dist in range(1, depth):
        planes(dist, corner)
        planes(dist + 1, sides)
        planes(dist, whole)
        planes(dist + 3, column)

    parts = []
    for t in range(count):
        home = owners[t] * n_aux + blocks[t] // own
        near = got[home, arows:, :].astype(F32)
        row = jnp.sum(jnp.where(iota(near.shape, 0) == blocks[t] % own, near, 0.0), axis=0, keepdims=True)
        parts.append(jnp.where(diag, row, 0.0))
    square = dot(jnp.concatenate(parts, axis=0).astype(BF16), fold_minor)
    vir_rep[...] = jnp.concatenate([square] * (pairs // 128), axis=1).reshape(vir_rep.shape)

    def tile(t, carry):
        acc = jnp.zeros((BS, pairs), F32)
        lines = []
        for first in range(0, pairs, CHUNK):
            gram = dot_nt(cbuf[t, first : first + CHUNK, :], tbuf[t])
            for at in range(CHUNK // BS):
                i = first // BS + at
                block_i = gram[at * BS : (at + 1) * BS, :]
                acc = acc + block_i * occ_rep[t, i : i + 1, :]
                lines.append(jnp.sum(block_i * vir_rep[t], axis=0, keepdims=True))
        vir_sums[t] = acc
        occ_sums[t] = jnp.concatenate(lines, axis=0)
        return carry

    lax.fori_loop(0, count, tile, 0)

    def flatten(mat, folding):
        high = mat.astype(BF16)
        low = (mat - high.astype(F32)).astype(BF16)
        both = dot(high, folding) + dot(low, folding)
        lines = []
        for t in range(count):
            wide = jnp.concatenate([both[t * BS : (t + 1) * BS]] * (pairs // 128), axis=1)
            lines.append(jnp.sum(jnp.where(diag, wide, 0.0), axis=0, keepdims=True))
        return lines

    vir_flat = flatten(vir_sums[...].reshape(count * BS, pairs), fold_minor)
    shape = (n_dev, own, 1)
    place_id = iota(shape, 0) * own + iota(shape, 1)
    total = jnp.zeros(vir_send.shape, F32)
    for t in range(count):
        hot = (place_id == owners[t] * (n_aux * own) + blocks[t]).astype(F32)
        total = total + hot * vir_flat[t].reshape(1, 1, pairs)
    vir_send[...] = total.astype(BF16)
    occ_flat = flatten(occ_sums[...].reshape(count * BS, pairs), fold(False, pairs))
    shape = (n_aux, own, 1)
    place_id = iota(shape, 0) * own + iota(shape, 1)
    total = jnp.zeros(occ_send.shape, F32)
    for t in range(count):
        hot = (place_id == rows[t]).astype(F32)
        total = total + hot * occ_flat[t].reshape(1, 1, pairs)
    occ_send[...] = total

    trade(
        n_blk, n_aux, norm, sizes, occ_send, vir_send, occ_out, vir_out, occ_got, vir_got, occ_sems, vir_sems
    )

    for zz in range(depth):
        block = ident(x, y, zz, c)
        for way in (over_x, over_y, mate):
            copy(way, block).wait_send()

        @pl.when((zz <= z) & has_up)
        def _():
            copy(up, ident(x, y, zz, c)).wait_send()

        @pl.when((zz >= z) & has_down)
        def _():
            copy(down, ident(x, y, zz, c)).wait_send()

        block = ident(1 - x, y, zz, c)
        copy(mate, block).wait_send()
        if zz % 2 == 0:
            copy(over_y, block).wait_send()
        block = ident(x, 1 - y, zz, c)
        copy(mate, block).wait_send()
        if zz % 2 == 1:
            copy(over_x, block).wait_send()
        copy(mate, ident(1 - x, 1 - y, zz, c)).wait_send()


def fused(sizes, rows, owners, blocks, adj, occ, vir, three, n_blk, n_aux, norm):
    n_dev = n_blk * n_aux
    count, pairs, naux = three.shape
    own = occ.shape[0] // n_aux
    smem = pl.BlockSpec(memory_space=pltpu.SMEM)
    vmem = pl.BlockSpec(memory_space=pltpu.VMEM)
    square = pltpu.VMEM((count, BS, pairs), F32)
    return pl.pallas_call(
        functools.partial(fused_kernel, n_blk, n_aux, norm),
        out_shape=jax.ShapeDtypeStruct((2, own, pairs), F32),
        in_specs=[smem] * 4 + [vmem] * 3 + [pl.BlockSpec(memory_space=pl.ANY)],
        out_specs=vmem,
        scratch_shapes=[
            pltpu.VMEM((n_dev, adj.shape[0] + own, naux), BF16),
            pltpu.VMEM((count, pairs, naux), BF16),
            pltpu.VMEM((count, pairs, naux), BF16),
            square,
            square,
            square,
            square,
            pltpu.VMEM((n_aux, own, pairs), F32),
            pltpu.VMEM((n_dev, own, pairs), BF16),
            pltpu.VMEM((n_aux, own, pairs), F32),
            pltpu.VMEM((n_dev, own, pairs), BF16),
            pltpu.SemaphoreType.DMA((count,)),
            pltpu.SemaphoreType.DMA((5, n_dev)),
            pltpu.SemaphoreType.DMA((n_dev,)),
            pltpu.SemaphoreType.DMA((2, n_aux)),
            pltpu.SemaphoreType.DMA((2, n_dev)),
        ],
        compiler_params=pltpu.CompilerParams(
            collective_id=0, has_side_effects=True, vmem_limit_bytes=67043328
        ),
        name="fused",
    )(sizes, rows, owners, blocks, adj, occ, vir, three)


def tile_kernel(
    n_aux, own, sizes, rows, owners, blocks, occ_ref, vir_ref, adj_ref, t_ref, occ_out, vir_out, vir_acc
):
    t = pl.program_id(0)
    pairs = BS * BS
    naux = adj_ref.shape[0]

    @pl.when(t == 0)
    def _():
        occ_out[...] = jnp.zeros_like(occ_out)
        vir_acc[...] = jnp.zeros_like(vir_acc)

    row, owner, block = rows[t], owners[t], blocks[t]
    size = sizes[row]
    lane = iota((1, pairs), 1)
    inside = (lane // BS < size) & (lane % BS < size)
    occ_all = occ_ref[...].astype(F32)
    occ_row = jnp.sum(jnp.where(iota(occ_all.shape, 0) == row, occ_all, 0.0), axis=0, keepdims=True)
    occ_row = jnp.where(inside, occ_row, 0.0)
    home = owner * n_aux + block // own
    vir_all = vir_ref[home].astype(F32)
    vir_row = jnp.sum(jnp.where(iota(vir_all.shape, 0) == block % own, vir_all, 0.0), axis=0, keepdims=True)
    diag = iota((BS, pairs), 1) // BS == iota((BS, pairs), 0)
    fold_minor = (iota((pairs, 128), 0) % BS == iota((pairs, 128), 1) % BS).astype(BF16)
    fold_major = (iota((pairs, 128), 0) // BS == iota((pairs, 128), 1) % BS).astype(BF16)
    spread = (iota((128, pairs), 0) == iota((128, pairs), 1) // BS).astype(BF16)
    repeat = pairs // 128

    def square(flat):
        return jnp.dot(jnp.where(diag, flat, 0.0).astype(BF16), fold_minor, preferred_element_type=F32)

    occ_rep = jnp.dot(square(occ_row).astype(BF16), spread, preferred_element_type=F32)
    vir_rep = jnp.concatenate([square(vir_row)] * repeat, axis=1)

    nt = (((1,), (1,)), ((), ()))
    acc = jnp.zeros((BS, pairs), F32)
    lines = []
    for first in range(0, pairs, CHUNK):
        part = lax.dot_general(t_ref[0, first : first + CHUNK, :], adj_ref[...], nt, preferred_element_type=F32)
        gram = lax.dot_general(part.astype(BF16), t_ref[0], nt, preferred_element_type=F32)
        for at in range(CHUNK // BS):
            i = first // BS + at
            block_i = gram[at * BS : (at + 1) * BS, :]
            acc = acc + block_i * occ_rep[i : i + 1, :]
            lines.append(jnp.sum(block_i * vir_rep, axis=0, keepdims=True))
    zmat = jnp.concatenate(lines, axis=0)

    def flatten(mat, fold):
        high = mat.astype(BF16)
        low = (mat - high.astype(F32)).astype(BF16)
        both = jnp.dot(high, fold, preferred_element_type=F32) + jnp.dot(low, fold, preferred_element_type=F32)
        wide = jnp.concatenate([both] * repeat, axis=1)
        return jnp.sum(jnp.where(diag, wide, 0.0), axis=0, keepdims=True)

    occ_flat = flatten(zmat, fold_major)
    vir_flat = flatten(acc, fold_minor)
    slot = iota((own, pairs), 0)
    occ_out[row // own] = occ_out[row // own] + jnp.where(slot == row % own, occ_flat, 0.0)
    vir_acc[home] = vir_acc[home] + jnp.where(slot == block % own, vir_flat, 0.0)

    @pl.when(t == pl.num_programs(0) - 1)
    def _():
        vir_out[...] = vir_acc[...].astype(vir_out.dtype)


def tiles(sizes, rows, owners, blocks, occ, vir, adj, three, n_dev, n_aux):
    count, pairs, naux = three.shape
    own = occ.shape[0] // n_aux
    smem = pl.BlockSpec(memory_space=pltpu.SMEM)
    vmem = pl.BlockSpec(memory_space=pltpu.VMEM)
    return pl.pallas_call(
        functools.partial(tile_kernel, n_aux, own),
        grid=(count,),
        out_shape=(
            jax.ShapeDtypeStruct((n_aux, own, pairs), F32),
            jax.ShapeDtypeStruct((n_dev, own, pairs), BF16),
        ),
        in_specs=[smem] * 4 + [vmem] * 3 + [pl.BlockSpec((1, pairs, naux), lambda t: (t, 0, 0))],
        out_specs=(vmem, vmem),
        scratch_shapes=[pltpu.VMEM((n_dev, own, pairs), F32)],
        compiler_params=pltpu.CompilerParams(vmem_limit_bytes=48 * 1024 * 1024),
        name="tiles",
    )(sizes, rows, owners, blocks, occ, vir, adj, three)


def exchange_kernel(
    n_blk, n_aux, norm, sizes, occ_ref, vir_ref, occ_out, vir_out, occ_got, vir_got, occ_sems, vir_sems
):
    n_dev = n_blk * n_aux
    b = lax.axis_index("blk")
    a = lax.axis_index("aux")
    me = b * n_aux + a
    barrier = pltpu.get_barrier_semaphore()

    def greet(k, carry):
        p = lax.rem(me + k, n_dev)
        pl.semaphore_signal(barrier, inc=1, device_id=(p // n_aux, p % n_aux), device_id_type=MESH)
        return carry

    lax.fori_loop(1, n_dev, greet, 0)
    pl.semaphore_wait(barrier, n_dev - 1)

    trade(n_blk, n_aux, norm, sizes, occ_ref, vir_ref, occ_out, vir_out, occ_got, vir_got, occ_sems, vir_sems)


def trade(n_blk, n_aux, norm, sizes, occ_ref, vir_ref, occ_out, vir_out, occ_got, vir_got, occ_sems, vir_sems):
    n_dev = n_blk * n_aux
    b = lax.axis_index("blk")
    a = lax.axis_index("aux")
    me = b * n_aux + a
    own, pairs = occ_out.shape

    def vir_copy(k, source):
        p = lax.rem(me + k, n_dev)
        return pltpu.make_async_remote_copy(
            src_ref=vir_ref.at[p],
            dst_ref=vir_got.at[source],
            send_sem=vir_sems.at[0, k],
            recv_sem=vir_sems.at[1, source],
            device_id=(p // n_aux, p % n_aux),
            device_id_type=MESH,
        )

    def occ_copy(k, source):
        q = lax.rem(a + k, n_aux)
        return pltpu.make_async_remote_copy(
            src_ref=occ_ref.at[q],
            dst_ref=occ_got.at[source],
            send_sem=occ_sems.at[0, k],
            recv_sem=occ_sems.at[1, source],
            device_id=(b, q),
            device_id_type=MESH,
        )

    def start_vir(k, carry):
        vir_copy(k, me).start()
        return carry

    def start_occ(k, carry):
        occ_copy(k, a).start()
        return carry

    lax.fori_loop(1, n_dev, start_vir, 0)
    lax.fori_loop(1, n_aux, start_occ, 0)

    def take_vir(k, total):
        source = lax.rem(me + k, n_dev)
        vir_copy(k, source).wait_recv()
        return total + vir_got[source].astype(F32)

    def take_occ(k, total):
        source = lax.rem(a + k, n_aux)
        occ_copy(k, source).wait_recv()
        return total + occ_got[source]

    occ_sum = lax.fori_loop(1, n_aux, take_occ, occ_ref[a])
    vir_sum = lax.fori_loop(1, n_dev, take_vir, vir_ref[me].astype(F32))
    lane = iota((1, pairs), 1)
    for r in range(own):
        size = sizes[a * own + r]
        scale = jnp.where((lane // BS < size) & (lane % BS < size), norm, 0.0).astype(F32)
        occ_out[r : r + 1, :] = occ_sum[r : r + 1, :] * scale
        vir_out[r : r + 1, :] = vir_sum[r : r + 1, :] * scale

    def end_vir(k, carry):
        vir_copy(k, me).wait_send()
        return carry

    def end_occ(k, carry):
        occ_copy(k, a).wait_send()
        return carry

    lax.fori_loop(1, n_dev, end_vir, 0)
    lax.fori_loop(1, n_aux, end_occ, 0)


def exchange(sizes, occ, vir, n_blk, n_aux, norm):
    n_dev, own, pairs = vir.shape
    vmem = pl.BlockSpec(memory_space=pltpu.VMEM)
    out = jax.ShapeDtypeStruct((own, pairs), F32)
    return pl.pallas_call(
        functools.partial(exchange_kernel, n_blk, n_aux, norm),
        out_shape=(out, out),
        in_specs=[pl.BlockSpec(memory_space=pltpu.SMEM), vmem, vmem],
        out_specs=(vmem, vmem),
        scratch_shapes=[
            pltpu.VMEM(occ.shape, occ.dtype),
            pltpu.VMEM(vir.shape, vir.dtype),
            pltpu.SemaphoreType.DMA((2, n_aux)),
            pltpu.SemaphoreType.DMA((2, n_dev)),
        ],
        compiler_params=pltpu.CompilerParams(collective_id=1, has_side_effects=True),
        name="exchange",
    )(sizes, occ, vir)


def shards(
    n_blk, n_aux, adjoint, three_centre, occ_density, vir_density, block_sizes, tile_rows, col_owner, col_block
):
    n_dev = n_blk * n_aux
    count = three_centre.shape[0]
    naux = three_centre.shape[3]
    own = occ_density.shape[0] // n_aux
    depth = adjoint.shape[0]
    three = three_centre.reshape(count, BS * BS, naux)
    if n_aux == 4 and n_blk % 2 == 0:
        both = fused(
            block_sizes, tile_rows, col_owner.reshape(count), col_block, adjoint, occ_density, vir_density,
            three, n_blk, n_aux, naux ** -0.5,
        )
        return both[0], both[1]
    aux_here = lax.axis_index("aux")
    own_sizes = lax.dynamic_slice_in_dim(block_sizes, aux_here * own, own, 0)
    own_vir = lax.dynamic_slice_in_dim(vir_density, aux_here * own, own, 0)
    lane = jnp.arange(BS * BS, dtype=jnp.int32)[None, :]
    inside = (lane // BS < own_sizes[:, None]) & (lane % BS < own_sizes[:, None])
    own_vir = jnp.where(inside, own_vir, jnp.zeros_like(own_vir))
    got = lax.all_gather(jnp.concatenate((adjoint, own_vir), axis=0), ("blk", "aux"), axis=0)
    adj = got[:, :depth, :].reshape(naux, naux)
    vir = got[:, depth:, :]
    occ_terms, vir_terms = tiles(
        block_sizes, tile_rows, col_owner.reshape(count), col_block, occ_density, vir, adj,
        three, n_dev, n_aux,
    )
    return exchange(block_sizes, occ_terms, vir_terms, n_blk, n_aux, naux ** -0.5)


def solution(mesh):
    in_specs = (
        P(("blk", "aux"), None),
        P(("blk", "aux"), None, None, None),
        P("blk", None),
        P("blk", None),
        P("blk"),
        P(("blk", "aux")),
        P(("blk", "aux"), None),
        P(("blk", "aux")),
    )
    out_specs = (P(("blk", "aux"), None), P(("blk", "aux"), None))
    body = functools.partial(shards, mesh.shape["blk"], mesh.shape["aux"])
    return jax.shard_map(body, mesh=mesh, in_specs=in_specs, out_specs=out_specs, check_vma=False)
```
